32 devices in a mesh: tm: 8 (over z, x), col: 4 (over y, core).
Axes of the slice: x: 2, y: 2, z: 4, core: 2. Of those that a mesh axis runs over, the one named last changes fastest.
Arguments:
- design: float32 [4096, 32768], P('tm', 'col'), may hold values from -6 to 6
- fir_taps: float32 [128], replicated, may hold values from -0.5 to 0.5
- column_block: int32 [128], replicated, may hold values from 0 to 127, each once
- panels: int32 [2], replicated, may hold values from 0 to 127, as said below
Outputs:
- normal_rows: float32 [2, 256, 32768], P(None, 'tm', 'col')
The draws below stay inside these ranges and needn't reach their ends.
Inputs may be any that keep to these rules, and one draw needn't show every extreme that they name: column_block is a permutation of the block numbers. `panels`: the two entries differ; one of them is the last block number 128 - 1.
All inputs are finite; a program needn't handle non-finite values.
Results may differ from the reference program's by a relative error of at most 0.0001.
Values sent between devices are 32-bit elements; how exact they have to be, the bound alone decides.
A program may use at most 128 MiB of HBM per device.

```python
import jax
import jax.numpy as jnp
from jax import lax

NCOL = 32768
PANEL = 256
TAPS = 128
EPOCHS = 4096
NBLK = 128


def draw_panels(key, part):
    block_total = NCOL // PANEL
    top_block = jnp.full((), block_total - 1, jnp.int32)
    other_block = jax.random.randint(jax.random.fold_in(key, 7), (), 0, block_total - 1).astype(jnp.int32)
    slot_pick = jax.random.randint(jax.random.fold_in(key, 11), (), 0, 2).astype(jnp.int32)
    first = jnp.where(slot_pick == 0, top_block, other_block)
    second = jnp.where(slot_pick == 0, other_block, top_block)
    return jnp.stack([first, second]).astype(jnp.int32)


def block_scale(own_key, shape, cuts, least, high):
    def one(dim, shards_of):
        heights = jax.random.uniform(jax.random.fold_in(jax.random.fold_in(own_key, 6), dim), (shards_of,), jnp.float32, least / len(cuts), high / len(cuts))
        return jnp.repeat(jnp.exp(heights), shape[dim] // shards_of).reshape((-1,) + (1,) * (len(shape) - dim - 1))

    factor_of = one(*cuts[0])
    for cut in cuts[1:]:
        factor_of = factor_of * one(*cut)
    return factor_of


def scatter_about(rng, shape, scale, most, split=(), kind=jnp.bfloat16):
    gain = block_scale(rng, shape, split, -0.22, 0.18) if split else 1.0
    entries = jax.random.normal(rng, shape, jnp.float32) * scale * gain
    return jnp.minimum(jnp.maximum(entries, -most), most).astype(kind)


def setup_inputs(seed: int = 0) -> dict:
    key_of = jax.random.split(jax.random.key(seed), 5)
    return {
        "design": scatter_about(key_of[0], (EPOCHS, NCOL), 1.0, 6.0, ((0, 8), (1, 4)), jnp.float32),
        "fir_taps": scatter_about(key_of[1], (TAPS,), TAPS ** -0.5, 0.5, (), jnp.float32),
        "column_block": jax.random.permutation(key_of[2], NCOL // PANEL).astype(jnp.int32),
        "panels": draw_panels(jax.random.fold_in(key_of[4], 71), 0),
    }


def fir_matrices(fir_taps):
    tap_count = fir_taps.shape[0]
    lag_index = jnp.arange(tap_count, dtype=jnp.int32)[:, None] - jnp.arange(tap_count, dtype=jnp.int32)[None, :]
    current = jnp.where(lag_index >= 0, fir_taps[jnp.clip(lag_index, 0, tap_count - 1)], jnp.zeros((), fir_taps.dtype))
    previous = jnp.where(lag_index < 0, fir_taps[jnp.clip(lag_index + tap_count, 0, tap_count - 1)], jnp.zeros((), fir_taps.dtype))
    return previous, current


def reference(design, fir_taps, column_block, panels):
    row_count, col_width = design.shape
    previous, current = fir_matrices(fir_taps)
    extended = jnp.concatenate([jnp.zeros((TAPS, col_width), design.dtype), design], axis=0)
    extended = extended.reshape(row_count // TAPS + 1, TAPS, col_width)
    filtered = jnp.einsum("rs,bsc->brc", previous, extended[:-1], precision=lax.Precision.HIGHEST, preferred_element_type=jnp.float32)
    filtered = filtered + jnp.einsum("rs,bsc->brc", current, extended[1:], precision=lax.Precision.HIGHEST, preferred_element_type=jnp.float32)
    filtered = filtered.reshape(row_count, col_width)
    block_ids = jnp.arange(NBLK, dtype=jnp.int32)
    results = []
    for panel_slot in range(2):
        target = panels[panel_slot]
        position = jnp.sum(jnp.where(column_block == target, block_ids, 0)).astype(jnp.int32)
        panel_cols = lax.dynamic_slice_in_dim(filtered, (position * PANEL).astype(jnp.int32), PANEL, 1)
        gram = lax.dot_general(panel_cols, filtered, (((0,), (0,)), ((), ())), precision=lax.Precision.HIGHEST, preferred_element_type=jnp.float32)
        upper_mask = jnp.repeat((column_block >= target).astype(jnp.float32), PANEL)
        results.append(gram * upper_mask[None, :] / EPOCHS)
    return jnp.stack(results, axis=0)
```

```python
import functools

import jax
import jax.numpy as jnp
from jax import lax
from jax.experimental import pallas as pl
from jax.experimental.pallas import tpu as pltpu
from jax.sharding import PartitionSpec as P

PANEL = 256
STEP = 8
MESH = pl.DeviceIdType.MESH
HIGHEST = lax.Precision.HIGHEST
f32, bf16 = jnp.float32, jnp.bfloat16


def split(x):
    hi = x.astype(bf16)
    return hi, (x - hi.astype(f32)).astype(bf16)


def dot(a, b, precision=None):
    return jnp.dot(a, b, precision=precision, preferred_element_type=f32)


def filter_kernel(last_ref, taps_ref, before_ref, sel_ref, after_ref, wt_ref, gram_ref, y_ref, w_ref):
    taps = taps_ref.shape[1] // 2
    rows, cols = sel_ref.shape
    blocks = rows // taps
    forward = pltpu.roll(jnp.broadcast_to(taps_ref[0:1, :], (taps, 2 * taps)), 0, 1, stride=1, stride_axis=0)
    adjoint = pltpu.roll(jnp.broadcast_to(taps_ref[1:2, :], (taps, 2 * taps)), 0, 1, stride=1, stride_axis=0)
    for b in range(blocks + 1):
        low = before_ref[...] if b == 0 else sel_ref[(b - 1) * taps : b * taps, :]
        high = after_ref[...] if b == blocks else sel_ref[b * taps : (b + 1) * taps, :]
        y = dot(forward[:, :taps], low, HIGHEST) + dot(forward[:, taps:], high, HIGHEST)
        if b == blocks:
            y = jnp.where(last_ref[0] != 0, 0.0, y)
        y_ref[b * taps : (b + 1) * taps, :] = y
    for b in range(blocks):
        w_ref[b * taps : (b + 1) * taps, :] = dot(adjoint, y_ref[b * taps : (b + 2) * taps, :], HIGHEST)
    wt_ref[...] = w_ref[:, :PANEL].T
    gram_ref[...] = dot(w_ref[:, PANEL:].T, sel_ref[:, PANEL:], HIGHEST)


def product_kernel(count, index_ref, wt_ref, gram_ref, d_ref, o_ref):
    k = pl.program_id(0)

    @pl.when(k < count)
    def _():
        whi, wlo = split(wt_ref[...])
        dhi, dlo = split(d_ref[...])
        o_ref[0] = dot(whi, dhi) + (dot(whi, dlo) + dot(wlo, dhi))

    @pl.when(k == count)
    def _():
        o_ref[0] = gram_ref[...]


def scatter_kernel(levels, pieces, p_ref, o_ref, *rest):
    bufs, (send_sem, recv_sem) = rest[:levels], rest[levels:]
    me = lax.axis_index("tm")
    bits = [(me // (1 << s)) % 2 for s in range(levels)]
    partners = [me + (1 - 2 * bits[s]) * (1 << s) for s in range(levels)]

    barrier = pltpu.get_barrier_semaphore()
    for s in range(levels):
        pl.semaphore_signal(barrier, inc=1, device_id={"tm": partners[s]}, device_id_type=MESH)
    pl.semaphore_wait(barrier, levels)

    def part(ref, s, g, bit):
        return (g,) + (slice(None),) * (levels - s - 1) + (bit,)

    def copy(s, g):
        src = p_ref if s == 0 else bufs[s - 1]
        return pltpu.make_async_remote_copy(
            src_ref=src.at[part(src, s, g, 1 - bits[s])],
            dst_ref=bufs[s].at[g],
            send_sem=send_sem.at[s, g],
            recv_sem=recv_sem.at[s, g],
            device_id={"tm": partners[s]},
            device_id_type=MESH,
        )

    def add(s, g):
        copy(s, g).wait_recv()
        src = p_ref if s == 0 else bufs[s - 1]
        total = bufs[s][g] + src[part(src, s, g, bits[s])]
        if s == levels - 1:
            o_ref[g] = total
        else:
            bufs[s][g] = total
            copy(s + 1, g).start()

    lag = 2

    @pl.loop(0, pieces)
    def _(g):
        copy(0, g).start()

    @pl.loop(0, pieces + lag * (levels - 1))
    def _(i):
        for s in range(levels):
            g = i - lag * s

            @pl.when(jnp.logical_and(g >= 0, g < pieces))
            def _():
                add(s, g)

    @pl.loop(0, pieces)
    def _(g):
        for s in range(levels):
            copy(s, g).wait_send()


def place_kernel(epochs, slot_ref, active_ref, is_last_ref, jp_ref, r_ref, o_ref):
    blocks = slot_ref.shape[0]
    pieces = r_ref.shape[0]
    jp = jp_ref[0]

    @pl.loop(0, blocks)
    def _(b):
        cols = pl.ds(pl.multiple_of(b * PANEL, PANEL), PANEL)
        o_ref[jp, :, cols] = jnp.where(active_ref[b] != 0, r_ref[slot_ref[b]] / epochs, 0.0)
        o_ref[1 - jp, :, cols] = jnp.where(is_last_ref[b] != 0, r_ref[pieces - 1] / epochs, 0.0)


def vmem():
    return pl.BlockSpec(memory_space=pltpu.VMEM)


def smem():
    return pl.BlockSpec(memory_space=pltpu.SMEM)


def params(**kw):
    return pltpu.CompilerParams(vmem_limit_bytes=56 * 2**20, **kw)


def product(count, index, wt, gram, design):
    rows = design.shape[0]
    pieces = count + 1
    return pl.pallas_call(
        functools.partial(product_kernel, count),
        out_shape=jax.ShapeDtypeStruct((pieces, PANEL, PANEL), f32),
        grid_spec=pltpu.PrefetchScalarGridSpec(
            num_scalar_prefetch=1,
            grid=(pieces,),
            in_specs=[
                pl.BlockSpec((PANEL, rows), lambda k, i: (0, 0)),
                pl.BlockSpec((PANEL, PANEL), lambda k, i: (0, 0)),
                pl.BlockSpec((rows, PANEL), lambda k, i: (0, i[k])),
            ],
            out_specs=pl.BlockSpec((1, PANEL, PANEL), lambda k, i: (k, 0, 0)),
        ),
        compiler_params=params(),
        name=f"product_{count}",
    )(index, wt, gram, design)


def scatter(partial, n, cid):
    pieces = partial.shape[0]
    share = PANEL // n
    levels = n.bit_length() - 1
    partial = partial.reshape((pieces,) + (2,) * levels + (share, PANEL))
    return pl.pallas_call(
        functools.partial(scatter_kernel, levels, pieces),
        out_shape=jax.ShapeDtypeStruct((pieces, share, PANEL), f32),
        in_specs=[vmem()],
        out_specs=vmem(),
        scratch_shapes=[
            pltpu.VMEM((pieces,) + (2,) * (levels - s - 1) + (share, PANEL), f32) for s in range(levels)
        ]
        + [pltpu.SemaphoreType.DMA((levels, pieces)), pltpu.SemaphoreType.DMA((levels, pieces))],
        compiler_params=params(collective_id=cid, has_side_effects=True),
        name=f"scatter_{pieces}",
    )(partial)


def swapped(x, axis, distance):
    n = lax.axis_size(axis)
    return lax.ppermute(x, axis, [(i, i ^ distance) for i in range(n)])


def over_col(x):
    n = lax.axis_size("col")
    if n == 1:
        return x
    rows = x.shape[0]
    odd = lax.axis_index("col") % 2
    x = x + swapped(x, "col", 1)
    if n == 2:
        return x
    half = lax.dynamic_slice_in_dim(x, odd * (rows // 2), rows // 2, 0)
    distance = 2
    while distance < n:
        half = half + swapped(half, "col", distance)
        distance *= 2
    other = swapped(half, "col", 1)
    return jnp.concatenate([jnp.where(odd == 0, half, other), jnp.where(odd == 0, other, half)], axis=0)


def shards(design, fir_taps, column_block, panels):
    rows, width = design.shape
    taps = fir_taps.shape[0]
    block_total = column_block.shape[0]
    blocks = width // PANEL
    n = lax.axis_size("tm")
    groups = lax.axis_size("col")
    group = lax.axis_index("col")
    time = lax.axis_index("tm")
    epochs = rows * n

    jp = jnp.where(panels[0] == block_total - 1, 1, 0).astype(jnp.int32)
    target = jnp.where(jp == 0, panels[0], panels[1])
    ids = jnp.arange(block_total, dtype=jnp.int32)
    chosen = []
    for wanted in (target, jnp.int32(block_total - 1)):
        position = jnp.sum(jnp.where(column_block == wanted, ids, 0))
        local = position - group * blocks
        mine = jnp.logical_and(local >= 0, local < blocks)
        block = lax.dynamic_slice_in_dim(design, jnp.clip(local, 0, blocks - 1) * PANEL, PANEL, 1)
        chosen.append(jnp.where(mine, block, 0.0))
    sel = jnp.concatenate(chosen, axis=1)
    before = lax.ppermute(sel[rows - taps :], "tm", [(i, i + 1) for i in range(n - 1)])
    after = lax.ppermute(sel[:taps], "tm", [(i + 1, i) for i in range(n - 1)])
    zeros = jnp.zeros((taps,), f32)
    forward = jnp.concatenate([zeros[:1], fir_taps[::-1], zeros[1:]])
    adjoint = jnp.concatenate([fir_taps, zeros])
    last = (time == n - 1).astype(jnp.int32)[None]
    wt, gram = pl.pallas_call(
        filter_kernel,
        out_shape=(jax.ShapeDtypeStruct((PANEL, rows), f32), jax.ShapeDtypeStruct((PANEL, PANEL), f32)),
        in_specs=[smem(), vmem(), vmem(), vmem(), vmem()],
        out_specs=(vmem(), vmem()),
        scratch_shapes=[pltpu.VMEM((rows + taps, 2 * PANEL), f32), pltpu.VMEM((rows, 2 * PANEL), f32)],
        compiler_params=params(),
        name="filter_panels",
    )(last, jnp.stack([forward, adjoint]), before, sel, after)
    wt = over_col(wt)

    active = (column_block >= target).astype(jnp.int32)
    most = jnp.max(jnp.sum(active.reshape(groups, blocks), axis=1))
    own = lax.dynamic_slice_in_dim(column_block, group * blocks, blocks, 0)
    own_active = (own >= target).astype(jnp.int32)
    own_last = (own == block_total - 1).astype(jnp.int32)
    local_ids = jnp.arange(blocks, dtype=jnp.int32)
    slot = jnp.sum(jnp.where(local_ids[None, :] < local_ids[:, None], own_active[None, :], 0), axis=1)
    hit = jnp.logical_and(slot[None, :] == jnp.arange(blocks + 1)[:, None], own_active[None, :] != 0)
    index = jnp.sum(jnp.where(hit, local_ids[None, :], 0), axis=1).astype(jnp.int32)
    slot = jnp.where(own_active != 0, slot, 0).astype(jnp.int32)

    counts = [min(c, blocks) for c in range(STEP, blocks + STEP, STEP)]

    def branch(order, count, index, wt, gram, design, slot, own_active, own_last, jp):
        partial = product(count, index[: count + 1], wt, gram, design)
        own_rows = scatter(partial, n, order)
        return pl.pallas_call(
            functools.partial(place_kernel, epochs),
            out_shape=jax.ShapeDtypeStruct((2, PANEL // n, width), f32),
            in_specs=[smem()] * 4 + [vmem()],
            out_specs=vmem(),
            compiler_params=params(),
            name=f"place_{count}",
        )(slot, own_active, own_last, jp[None], own_rows)

    pick = jnp.clip((most + STEP - 1) // STEP - 1, 0, len(counts) - 1)
    return lax.switch(
        pick,
        [functools.partial(branch, i, c) for i, c in enumerate(counts)],
        index, wt, gram, design, slot, own_active, own_last, jp,
    )


def solution(mesh):
    return jax.shard_map(
        shards,
        mesh=mesh,
        in_specs=(P("tm", "col"), P(), P(), P()),
        out_specs=P(None, "tm", "col"),
        check_vma=False,
    )
```

```python
import functools

import jax
import jax.numpy as jnp
from jax import lax
from jax.experimental import pallas as pl
from jax.experimental.pallas import tpu as pltpu
from jax.sharding import PartitionSpec as P

PANEL = 256
STEP = 4
LAG = 2
MESH = pl.DeviceIdType.MESH
HIGHEST = lax.Precision.HIGHEST
f32, bf16 = jnp.float32, jnp.bfloat16


def split(x):
    hi = x.astype(bf16)
    return hi, (x - hi.astype(f32)).astype(bf16)


def dot(a, b, precision=None):
    return jnp.dot(a, b, precision=precision, preferred_element_type=f32)


def filter_kernel(last_ref, taps_ref, before_ref, sel_ref, after_ref, wt_ref, gram_ref, y_ref, w_ref):
    taps = taps_ref.shape[1] // 2
    rows, cols = sel_ref.shape
    blocks = rows // taps
    forward = pltpu.roll(jnp.broadcast_to(taps_ref[0:1, :], (taps, 2 * taps)), 0, 1, stride=1, stride_axis=0)
    adjoint = pltpu.roll(jnp.broadcast_to(taps_ref[1:2, :], (taps, 2 * taps)), 0, 1, stride=1, stride_axis=0)
    for b in range(blocks + 1):
        low = before_ref[...] if b == 0 else sel_ref[(b - 1) * taps : b * taps, :]
        high = after_ref[...] if b == blocks else sel_ref[b * taps : (b + 1) * taps, :]
        y = dot(forward[:, :taps], low, HIGHEST) + dot(forward[:, taps:], high, HIGHEST)
        if b == blocks:
            y = jnp.where(last_ref[0] != 0, 0.0, y)
        y_ref[b * taps : (b + 1) * taps, :] = y
    for b in range(blocks):
        w_ref[b * taps : (b + 1) * taps, :] = dot(adjoint, y_ref[b * taps : (b + 2) * taps, :], HIGHEST)
    wt_ref[...] = w_ref[:, :PANEL].T
    gram_ref[...] = dot(w_ref[:, PANEL:].T, sel_ref[:, PANEL:], HIGHEST)


def rows_kernel(levels, count, index_ref, wt_ref, gram_ref, d_hbm, o_ref, d_ref, p_ref, whi_ref, wlo_ref, *rest):
    bufs, (load_sem, send_sem, recv_sem) = rest[:levels], rest[levels:]
    pieces = count + 1
    blocks = d_ref.shape[0]
    n = 1 << levels
    share = PANEL // n
    me = lax.axis_index("tm")
    bits = [(me // (1 << s)) % 2 for s in range(levels)]
    partners = [me + (1 - 2 * bits[s]) * (1 << s) for s in range(levels)]

    def load(c):
        cols = pl.ds(pl.multiple_of(c * PANEL, PANEL), PANEL)
        return pltpu.make_async_copy(d_hbm.at[:, cols], d_ref.at[c], load_sem.at[c])

    @pl.loop(0, blocks)
    def _(c):
        load(c).start()

    barrier = pltpu.get_barrier_semaphore()
    for s in range(levels):
        pl.semaphore_signal(barrier, inc=1, device_id={"tm": partners[s]}, device_id_type=MESH)
    whi_ref[...], wlo_ref[...] = split(wt_ref[...])

    @pl.loop(0, blocks)
    def _(c):
        load(c).wait()

    pl.semaphore_wait(barrier, levels)

    def other_order(g):
        return (g % 4) // 3 if levels > 1 else 0

    def bit_of(s, g):
        if s > 1 or levels == 1:
            return bits[s], partners[s]
        swap = other_order(g)
        return (
            bits[s] + swap * (bits[1 - s] - bits[s]),
            partners[s] + swap * (partners[1 - s] - partners[s]),
        )

    def part(s, g, bit):
        return (g,) + (slice(None),) * (levels - s - 1) + (bit,)

    def copy(s, g):
        src = p_ref if s == 0 else bufs[s - 1]
        bit, partner = bit_of(s, g)
        return pltpu.make_async_remote_copy(
            src_ref=src.at[part(s, g, 1 - bit)],
            dst_ref=bufs[s].at[g],
            send_sem=send_sem.at[s, g],
            recv_sem=recv_sem.at[s, g],
            device_id={"tm": partner},
            device_id_type=MESH,
        )

    def store(g, value):
        for i in range(n):
            at = [(i >> s) & 1 for s in reversed(range(levels))]
            rows_of = value[i * share : (i + 1) * share]
            if levels == 1:
                p_ref[(g, *at)] = rows_of
                continue
            first, second = at[-2], at[-1]
            swap = other_order(g)
            p_ref[(g, *at[:-2], first + swap * (second - first), second + swap * (first - second))] = rows_of

    def compute(g):
        @pl.when(g < count)
        def _():
            dhi, dlo = split(d_ref[index_ref[g]])
            whi = whi_ref[...]
            store(g, dot(whi, dhi) + (dot(whi, dlo) + dot(wlo_ref[...], dhi)))

        @pl.when(g == count)
        def _():
            store(g, gram_ref[...])

    def add(s, g):
        copy(s, g).wait_recv()
        src = p_ref if s == 0 else bufs[s - 1]
        total = bufs[s][g] + src[part(s, g, bit_of(s, g)[0])]
        if s == levels - 1:
            o_ref[g] = total
        else:
            bufs[s][g] = total
            copy(s + 1, g).start()

    @pl.loop(0, pieces + LAG * levels)
    def _(i):
        @pl.when(i < pieces)
        def _():
            compute(i)
            copy(0, i).start()

        for s in range(levels):
            g = i - LAG * (s + 1)

            @pl.when(jnp.logical_and(g >= 0, g < pieces))
            def _():
                add(s, g)

    @pl.loop(0, pieces)
    def _(g):
        for s in range(levels):
            copy(s, g).wait_send()


def place_kernel(epochs, slot_ref, active_ref, is_last_ref, jp_ref, r_ref, o_ref):
    blocks = slot_ref.shape[0]
    pieces = r_ref.shape[0]
    jp = jp_ref[0]

    @pl.loop(0, blocks)
    def _(b):
        cols = pl.ds(pl.multiple_of(b * PANEL, PANEL), PANEL)
        o_ref[jp, :, cols] = jnp.where(active_ref[b] != 0, r_ref[slot_ref[b]] / epochs, 0.0)
        o_ref[1 - jp, :, cols] = jnp.where(is_last_ref[b] != 0, r_ref[pieces - 1] / epochs, 0.0)


def vmem():
    return pl.BlockSpec(memory_space=pltpu.VMEM)


def smem():
    return pl.BlockSpec(memory_space=pltpu.SMEM)


def params(**kw):
    return pltpu.CompilerParams(vmem_limit_bytes=56 * 2**20, **kw)


def summed_rows(count, index, wt, gram, design, n, cid):
    pieces = count + 1
    rows = design.shape[0]
    blocks = design.shape[1] // PANEL
    share = PANEL // n
    levels = n.bit_length() - 1
    return pl.pallas_call(
        functools.partial(rows_kernel, levels, count),
        out_shape=jax.ShapeDtypeStruct((pieces, share, PANEL), f32),
        in_specs=[smem(), vmem(), vmem(), pl.BlockSpec(memory_space=pl.ANY)],
        out_specs=vmem(),
        scratch_shapes=[
            pltpu.VMEM((blocks, rows, PANEL), f32),
            pltpu.VMEM((pieces,) + (2,) * levels + (share, PANEL), f32),
            pltpu.VMEM((PANEL, rows), bf16),
            pltpu.VMEM((PANEL, rows), bf16),
        ]
        + [pltpu.VMEM((pieces,) + (2,) * (levels - s - 1) + (share, PANEL), f32) for s in range(levels)]
        + [
            pltpu.SemaphoreType.DMA((blocks,)),
            pltpu.SemaphoreType.DMA((levels, pieces)),
            pltpu.SemaphoreType.DMA((levels, pieces)),
        ],
        compiler_params=params(collective_id=cid, has_side_effects=True),
        name=f"rows_{count}",
    )(index, wt, gram, design)


def swapped(x, axis, distance):
    n = lax.axis_size(axis)
    return lax.ppermute(x, axis, [(i, i ^ distance) for i in range(n)])


def over_col(x):
    n = lax.axis_size("col")
    if n == 1:
        return x
    rows = x.shape[0]
    odd = lax.axis_index("col") % 2
    x = x + swapped(x, "col", 1)
    if n == 2:
        return x
    half = lax.dynamic_slice_in_dim(x, odd * (rows // 2), rows // 2, 0)
    distance = 2
    while distance < n:
        half = half + swapped(half, "col", distance)
        distance *= 2
    other = swapped(half, "col", 1)
    return jnp.concatenate([jnp.where(odd == 0, half, other), jnp.where(odd == 0, other, half)], axis=0)


def shards(design, fir_taps, column_block, panels):
    rows, width = design.shape
    taps = fir_taps.shape[0]
    block_total = column_block.shape[0]
    blocks = width // PANEL
    n = lax.axis_size("tm")
    groups = lax.axis_size("col")
    group = lax.axis_index("col")
    time = lax.axis_index("tm")
    epochs = rows * n

    jp = jnp.where(panels[0] == block_total - 1, 1, 0).astype(jnp.int32)
    target = jnp.where(jp == 0, panels[0], panels[1])
    ids = jnp.arange(block_total, dtype=jnp.int32)
    chosen = []
    for wanted in (target, jnp.int32(block_total - 1)):
        position = jnp.sum(jnp.where(column_block == wanted, ids, 0))
        local = position - group * blocks
        mine = jnp.logical_and(local >= 0, local < blocks)
        block = lax.dynamic_slice_in_dim(design, jnp.clip(local, 0, blocks - 1) * PANEL, PANEL, 1)
        chosen.append(jnp.where(mine, block, 0.0))
    sel = jnp.concatenate(chosen, axis=1)
    before = lax.ppermute(sel[rows - taps :], "tm", [(i, i + 1) for i in range(n - 1)])
    after = lax.ppermute(sel[:taps], "tm", [(i + 1, i) for i in range(n - 1)])
    zeros = jnp.zeros((taps,), f32)
    forward = jnp.concatenate([zeros[:1], fir_taps[::-1], zeros[1:]])
    adjoint = jnp.concatenate([fir_taps, zeros])
    last = (time == n - 1).astype(jnp.int32)[None]
    wt, gram = pl.pallas_call(
        filter_kernel,
        out_shape=(jax.ShapeDtypeStruct((PANEL, rows), f32), jax.ShapeDtypeStruct((PANEL, PANEL), f32)),
        in_specs=[smem(), vmem(), vmem(), vmem(), vmem()],
        out_specs=(vmem(), vmem()),
        scratch_shapes=[pltpu.VMEM((rows + taps, 2 * PANEL), f32), pltpu.VMEM((rows, 2 * PANEL), f32)],
        compiler_params=params(),
        name="filter_panels",
    )(last, jnp.stack([forward, adjoint]), before, sel, after)
    wt = over_col(wt)

    active = (column_block >= target).astype(jnp.int32)
    most = jnp.max(jnp.sum(active.reshape(groups, blocks), axis=1))
    own = lax.dynamic_slice_in_dim(column_block, group * blocks, blocks, 0)
    own_active = (own >= target).astype(jnp.int32)
    own_last = (own == block_total - 1).astype(jnp.int32)
    local_ids = jnp.arange(blocks, dtype=jnp.int32)
    slot = jnp.sum(jnp.where(local_ids[None, :] < local_ids[:, None], own_active[None, :], 0), axis=1)
    hit = jnp.logical_and(slot[None, :] == jnp.arange(blocks + 1)[:, None], own_active[None, :] != 0)
    index = jnp.sum(jnp.where(hit, local_ids[None, :], 0), axis=1).astype(jnp.int32)
    slot = jnp.where(own_active != 0, slot, 0).astype(jnp.int32)

    counts = [min(c, blocks) for c in range(STEP, blocks + STEP, STEP)]

    def branch(order, count, index, wt, gram, design, slot, own_active, own_last, jp):
        own_rows = summed_rows(count, index[: count + 1], wt, gram, design, n, order)
        return pl.pallas_call(
            functools.partial(place_kernel, epochs),
            out_shape=jax.ShapeDtypeStruct((2, PANEL // n, width), f32),
            in_specs=[smem()] * 4 + [vmem()],
            out_specs=vmem(),
            compiler_params=params(),
            name=f"place_{count}",
        )(slot, own_active, own_last, jp[None], own_rows)

    pick = jnp.clip((most + STEP - 1) // STEP - 1, 0, len(counts) - 1)
    return lax.switch(
        pick,
        [functools.partial(branch, i, c) for i, c in enumerate(counts)],
        index, wt, gram, design, slot, own_active, own_last, jp,
    )


def solution(mesh):
    return jax.shard_map(
        shards,
        mesh=mesh,
        in_specs=(P("tm", "col"), P(), P(), P()),
        out_specs=P(None, "tm", "col"),
        check_vma=False,
    )
```

```python
import functools

import jax
import jax.numpy as jnp
from jax import lax
from jax.experimental import pallas as pl
from jax.experimental.pallas import tpu as pltpu
from jax.sharding import PartitionSpec as P

PANEL = 256
STEP = 4
LAG = 2
MESH = pl.DeviceIdType.MESH
HIGHEST = lax.Precision.HIGHEST
f32, bf16 = jnp.float32, jnp.bfloat16


def split(x):
    hi = x.astype(bf16)
    return hi, (x - hi.astype(f32)).astype(bf16)


def dot(a, b, precision=None):
    return jnp.dot(a, b, precision=precision, preferred_element_type=f32)


def rows_kernel(levels, hops, count, index_ref, taps_ref, sel_ref, d_hbm, o_ref, d_ref, p_ref, whi_ref, wlo_ref, *rest):
    (before_ref, after_ref, y_ref, w_ref, wt_ref, mix_ref, came_ref, full_ref, gram_ref, band_ref), rest = rest[:10], rest[10:]
    bufs, (load_sem, halo_sem, col_send, col_recv, send_sem, recv_sem) = rest[:levels], rest[levels:]
    pieces = count + 1
    blocks = d_ref.shape[0]
    n = 1 << levels
    share = PANEL // n
    me = lax.axis_index("tm")
    group = lax.axis_index("col")
    bits = [(me // (1 << s)) % 2 for s in range(levels)]
    partners = [me + (1 - 2 * bits[s]) * (1 << s) for s in range(levels)]
    col_bits = [(group // (1 << s)) % 2 for s in range(hops)]
    col_partners = [group + (1 - 2 * col_bits[s]) * (1 << s) for s in range(hops)]
    taps = before_ref.shape[0]
    rows = sel_ref.shape[0]
    spans = rows // taps

    def load(c):
        cols = pl.ds(pl.multiple_of(c * PANEL, PANEL), PANEL)
        return pltpu.make_async_copy(d_hbm.at[:, cols], d_ref.at[c], load_sem.at[c])

    barrier = pltpu.get_barrier_semaphore()
    for s in range(levels):
        pl.semaphore_signal(barrier, inc=1, device_id={"tm": partners[s]}, device_id_type=MESH)
    for s in range(hops):
        pl.semaphore_signal(barrier, inc=1, device_id={"col": col_partners[s]}, device_id_type=MESH)

    for beside in (lax.rem(me + 1, n), lax.rem(me + n - 1, n)):
        pl.semaphore_signal(barrier, inc=1, device_id={"tm": beside}, device_id_type=MESH)
    pl.semaphore_wait(barrier, levels + hops + 2)

    def to_next():
        return pltpu.make_async_remote_copy(
            src_ref=sel_ref.at[rows - taps :],
            dst_ref=before_ref,
            send_sem=halo_sem.at[0],
            recv_sem=halo_sem.at[1],
            device_id={"tm": me + 1},
            device_id_type=MESH,
        )

    def to_previous():
        return pltpu.make_async_remote_copy(
            src_ref=sel_ref.at[:taps],
            dst_ref=after_ref,
            send_sem=halo_sem.at[2],
            recv_sem=halo_sem.at[3],
            device_id={"tm": me - 1},
            device_id_type=MESH,
        )

    @pl.when(me < n - 1)
    def _():
        to_next().start()

    @pl.when(me > 0)
    def _():
        to_previous().start()

    @pl.loop(0, blocks)
    def _(c):
        load(c).start()

    for i in range(2):
        lags = jnp.broadcast_to(taps_ref[i : i + 1, :], (taps, 2 * taps))
        band_ref[i] = pltpu.roll(lags, 0, 1, stride=1, stride_axis=0)

    def span(b, length=1):
        return pl.ds(pl.multiple_of(b * taps, taps), length * taps)

    def filtered(low, high):
        return dot(band_ref[0, :, :taps], low, HIGHEST) + dot(band_ref[0, :, taps:], high, HIGHEST)

    def inner(cols):
        @pl.loop(1, spans)
        def _(b):
            y_ref[span(b), cols] = dot(band_ref[0], sel_ref[span(b - 1, 2), cols], HIGHEST)

    def outer(cols):
        y_ref[:taps, cols] = filtered(before_ref[:, cols], sel_ref[:taps, cols])
        y_ref[rows:, cols] = filtered(sel_ref[rows - taps :, cols], after_ref[:, cols])

        @pl.when(me == n - 1)
        def _():
            y_ref[rows:, cols] = jnp.zeros((taps, PANEL), f32)

        @pl.loop(0, spans)
        def _(b):
            w_ref[span(b), cols] = dot(band_ref[1], y_ref[span(b, 2), cols], HIGHEST)

    first, second = slice(0, PANEL), slice(PANEL, 2 * PANEL)
    inner(first)

    @pl.when(me == 0)
    def _():
        before_ref[...] = jnp.zeros(before_ref.shape, f32)

    @pl.when(me > 0)
    def _():
        to_next().wait_recv()
        to_previous().wait_send()

    @pl.when(me == n - 1)
    def _():
        after_ref[...] = jnp.zeros(after_ref.shape, f32)

    @pl.when(me < n - 1)
    def _():
        to_next().wait_send()
        to_previous().wait_recv()

    outer(first)
    half = PANEL // 2
    wt = w_ref[:, first].T
    wt_ref[0] = wt[:half]
    wt_ref[1] = wt[half:]

    def hop(i, src, dst, s):
        return pltpu.make_async_remote_copy(
            src_ref=src,
            dst_ref=dst,
            send_sem=col_send.at[i],
            recv_sem=col_recv.at[i],
            device_id={"col": col_partners[s]},
            device_id_type=MESH,
        )

    if hops:
        own = col_bits[0]
        go = hop(0, wt_ref.at[1 - own], came_ref.at[0], 0)
        go.start()
        inner(second)
        go.wait_recv()
        mix_ref[0] = wt_ref[own] + came_ref[0]
        go.wait_send()
        for s in range(1, hops):
            go = hop(s, mix_ref.at[s - 1], came_ref.at[s], s)
            go.start()
            if s == 1:
                outer(second)
                gram_ref[...] = dot(w_ref[:, second].T, sel_ref[:, second], HIGHEST)
            go.wait_recv()
            mix_ref[s] = mix_ref[s - 1] + came_ref[s]
            go.wait_send()
        go = hop(hops, mix_ref.at[hops - 1], full_ref.at[own], 0)
        go.start()
        if hops == 1:
            outer(second)
            gram_ref[...] = dot(w_ref[:, second].T, sel_ref[:, second], HIGHEST)
        whi_ref[own], wlo_ref[own] = split(mix_ref[hops - 1])
        go.wait_recv()
        whi_ref[1 - own], wlo_ref[1 - own] = split(full_ref[1 - own])
        go.wait_send()
    else:
        inner(second)
        outer(second)
        gram_ref[...] = dot(w_ref[:, second].T, sel_ref[:, second], HIGHEST)
        whi_ref[...], wlo_ref[...] = split(wt_ref[...])

    @pl.loop(0, blocks)
    def _(c):
        load(c).wait()

    def other_order(g):
        return (g % 4) // 3 if levels > 1 else 0

    def bit_of(s, g):
        if s > 1 or levels == 1:
            return bits[s], partners[s]
        swap = other_order(g)
        return (
            bits[s] + swap * (bits[1 - s] - bits[s]),
            partners[s] + swap * (partners[1 - s] - partners[s]),
        )

    def part(s, g, bit):
        return (g,) + (slice(None),) * (levels - s - 1) + (bit,)

    def copy(s, g):
        src = p_ref if s == 0 else bufs[s - 1]
        bit, partner = bit_of(s, g)
        return pltpu.make_async_remote_copy(
            src_ref=src.at[part(s, g, 1 - bit)],
            dst_ref=bufs[s].at[g],
            send_sem=send_sem.at[s, g],
            recv_sem=recv_sem.at[s, g],
            device_id={"tm": partner},
            device_id_type=MESH,
        )

    def store(g, value):
        for i in range(n):
            at = [(i >> s) & 1 for s in reversed(range(levels))]
            rows_of = value[i * share : (i + 1) * share]
            if levels == 1:
                p_ref[(g, *at)] = rows_of
                continue
            first, second = at[-2], at[-1]
            swap = other_order(g)
            p_ref[(g, *at[:-2], first + swap * (second - first), second + swap * (first - second))] = rows_of

    def compute(g):
        @pl.when(g < count)
        def _():
            dhi, dlo = split(d_ref[index_ref[g]])
            whi = whi_ref[...].reshape(PANEL, rows)
            wlo = wlo_ref[...].reshape(PANEL, rows)
            store(g, dot(whi, dhi) + (dot(whi, dlo) + dot(wlo, dhi)))

        @pl.when(g == count)
        def _():
            store(g, gram_ref[...])

    def add(s, g):
        copy(s, g).wait_recv()
        src = p_ref if s == 0 else bufs[s - 1]
        total = bufs[s][g] + src[part(s, g, bit_of(s, g)[0])]
        if s == levels - 1:
            o_ref[g] = total
        else:
            bufs[s][g] = total
            copy(s + 1, g).start()

    @pl.loop(0, pieces + LAG * levels)
    def _(i):
        @pl.when(i < pieces)
        def _():
            compute(i)
            copy(0, i).start()

        for s in range(levels):
            g = i - LAG * (s + 1)

            @pl.when(jnp.logical_and(g >= 0, g < pieces))
            def _():
                add(s, g)

    @pl.loop(0, pieces)
    def _(g):
        for s in range(levels):
            copy(s, g).wait_send()


def place_kernel(epochs, slot_ref, active_ref, is_last_ref, jp_ref, r_ref, o_ref):
    blocks = slot_ref.shape[0]
    pieces = r_ref.shape[0]
    jp = jp_ref[0]

    @pl.loop(0, blocks)
    def _(b):
        cols = pl.ds(pl.multiple_of(b * PANEL, PANEL), PANEL)
        o_ref[jp, :, cols] = jnp.where(active_ref[b] != 0, r_ref[slot_ref[b]] / epochs, 0.0)
        o_ref[1 - jp, :, cols] = jnp.where(is_last_ref[b] != 0, r_ref[pieces - 1] / epochs, 0.0)


def vmem():
    return pl.BlockSpec(memory_space=pltpu.VMEM)


def smem():
    return pl.BlockSpec(memory_space=pltpu.SMEM)


def params(**kw):
    return pltpu.CompilerParams(vmem_limit_bytes=56 * 2**20, **kw)


def summed_rows(count, index, taps_pair, sel, design, n, groups, cid):
    pieces = count + 1
    rows = design.shape[0]
    blocks = design.shape[1] // PANEL
    taps = taps_pair.shape[1] // 2
    share = PANEL // n
    half = PANEL // 2
    levels = n.bit_length() - 1
    hops = groups.bit_length() - 1
    return pl.pallas_call(
        functools.partial(rows_kernel, levels, hops, count),
        out_shape=jax.ShapeDtypeStruct((pieces, share, PANEL), f32),
        in_specs=[smem(), vmem(), vmem(), pl.BlockSpec(memory_space=pl.ANY)],
        out_specs=vmem(),
        scratch_shapes=[
            pltpu.VMEM((blocks, rows, PANEL), f32),
            pltpu.VMEM((pieces,) + (2,) * levels + (share, PANEL), f32),
            pltpu.VMEM((2, half, rows), bf16),
            pltpu.VMEM((2, half, rows), bf16),
            pltpu.VMEM((taps, 2 * PANEL), f32),
            pltpu.VMEM((taps, 2 * PANEL), f32),
            pltpu.VMEM((rows + taps, 2 * PANEL), f32),
            pltpu.VMEM((rows, 2 * PANEL), f32),
            pltpu.VMEM((2, half, rows), f32),
            pltpu.VMEM((max(hops, 1), half, rows), f32),
            pltpu.VMEM((max(hops, 1), half, rows), f32),
            pltpu.VMEM((2, half, rows), f32),
            pltpu.VMEM((PANEL, PANEL), f32),
            pltpu.VMEM((2, taps, 2 * taps), f32),
        ]
        + [pltpu.VMEM((pieces,) + (2,) * (levels - s - 1) + (share, PANEL), f32) for s in range(levels)]
        + [
            pltpu.SemaphoreType.DMA((blocks,)),
            pltpu.SemaphoreType.DMA((4,)),
            pltpu.SemaphoreType.DMA((hops + 1,)),
            pltpu.SemaphoreType.DMA((hops + 1,)),
            pltpu.SemaphoreType.DMA((levels, pieces)),
            pltpu.SemaphoreType.DMA((levels, pieces)),
        ],
        compiler_params=params(collective_id=cid, has_side_effects=True),
        name=f"rows_{count}",
    )(index, taps_pair, sel, design)


def shards(design, fir_taps, column_block, panels):
    rows, width = design.shape
    taps = fir_taps.shape[0]
    block_total = column_block.shape[0]
    blocks = width // PANEL
    n = lax.axis_size("tm")
    groups = lax.axis_size("col")
    group = lax.axis_index("col")
    epochs = rows * n

    jp = jnp.where(panels[0] == block_total - 1, 1, 0).astype(jnp.int32)
    target = jnp.where(jp == 0, panels[0], panels[1])
    ids = jnp.arange(block_total, dtype=jnp.int32)
    chosen = []
    for wanted in (target, jnp.int32(block_total - 1)):
        position = jnp.sum(jnp.where(column_block == wanted, ids, 0))
        local = position - group * blocks
        mine = jnp.logical_and(local >= 0, local < blocks)
        block = lax.dynamic_slice_in_dim(design, jnp.clip(local, 0, blocks - 1) * PANEL, PANEL, 1)
        chosen.append(jnp.where(mine, block, 0.0))
    sel = jnp.concatenate(chosen, axis=1)
    zeros = jnp.zeros((taps,), f32)
    forward = jnp.concatenate([zeros[:1], fir_taps[::-1], zeros[1:]])
    adjoint = jnp.concatenate([fir_taps, zeros])
    taps_pair = jnp.stack([forward, adjoint])

    active = (column_block >= target).astype(jnp.int32)
    most = jnp.max(jnp.sum(active.reshape(groups, blocks), axis=1))
    own = lax.dynamic_slice_in_dim(column_block, group * blocks, blocks, 0)
    own_active = (own >= target).astype(jnp.int32)
    own_last = (own == block_total - 1).astype(jnp.int32)
    local_ids = jnp.arange(blocks, dtype=jnp.int32)
    slot = jnp.sum(jnp.where(local_ids[None, :] < local_ids[:, None], own_active[None, :], 0), axis=1)
    hit = jnp.logical_and(slot[None, :] == jnp.arange(blocks + 1)[:, None], own_active[None, :] != 0)
    index = jnp.sum(jnp.where(hit, local_ids[None, :], 0), axis=1).astype(jnp.int32)
    slot = jnp.where(own_active != 0, slot, 0).astype(jnp.int32)

    counts = [min(c, blocks) for c in range(STEP, blocks + STEP, STEP)]

    def branch(order, count, index, taps_pair, sel, design, slot, own_active, own_last, jp):
        own_rows = summed_rows(count, index[: count + 1], taps_pair, sel, design, n, groups, order)
        return pl.pallas_call(
            functools.partial(place_kernel, epochs),
            out_shape=jax.ShapeDtypeStruct((2, PANEL // n, width), f32),
            in_specs=[smem()] * 4 + [vmem()],
            out_specs=vmem(),
            compiler_params=params(),
            name=f"place_{count}",
        )(slot, own_active, own_last, jp[None], own_rows)

    pick = jnp.clip((most + STEP - 1) // STEP - 1, 0, len(counts) - 1)
    return lax.switch(
        pick,
        [functools.partial(branch, i, c) for i, c in enumerate(counts)],
        index, taps_pair, sel, design, slot, own_active, own_last, jp,
    )


def solution(mesh):
    return jax.shard_map(
        shards,
        mesh=mesh,
        in_specs=(P("tm", "col"), P(), P(), P()),
        out_specs=P(None, "tm", "col"),
        check_vma=False,
    )
```
